256 devices in a mesh: tm: 4 (over y), space: 64 (over x, z, core).
Axes of the slice: x: 4, y: 4, z: 8, core: 2. Of those that a mesh axis runs over, the one named last changes fastest.
Arguments:
- queries: bfloat16 [16, 4096, 1536], P('tm', 'space'), may hold values from -48 to 48
- key_rows: bfloat16 [16, 4096, 1536], P('tm', 'space'), may hold values from -4 to 4
- value_rows: bfloat16 [16, 4096, 1536], P('tm', 'space'), may hold values from -6 to 6
- dropout: int32 [4, 16, 4096, 12], P(None, 'tm', 'space'), may hold values 0 or 1
- tile_lists: int32 [64, 2], P('space'), may hold values from 0 to 63, as said below
Outputs:
- sampled_heads: bfloat16 [4, 16, 4096, 1536], P(None, 'tm', 'space')
The draws below stay inside these ranges and needn't reach their ends.
Inputs may be any that keep to these rules, and one draw needn't show every extreme that they name: `tile_lists`: row t holds t first and then (t - 1) or (t + 1) modulo 64.
All inputs are finite; a program needn't handle non-finite values. No bound on the sum of `dropout` on one device may be relied on, other than what follows from the above.
Results may differ from the reference program's by a relative error of at most 0.0045.
Values may be sent and summed in bfloat16 or wider, within the bound.
No kernel may reach another device: no remote copies, remote signals or barrier semaphores. Data moves between devices by JAX's collectives and lax.ppermute only.
A program may use at most 128 MiB of HBM per device.

```python
import math
import jax
import jax.numpy as jnp
from jax import lax

HEADS = 12
HEAD_DIM = 128
WIDTH = 1536
SAMPLES = 4
LIST_LEN = 2
TILE_TOK = 64
FRAMES = 16
TILES = 64
PIX = 4096


def paired_fields(key):
    base_key = jax.random.fold_in(key, 11)
    key_seed = jax.random.fold_in(base_key, 1)
    query_seed = jax.random.fold_in(base_key, 2)
    key_field = jnp.clip(jax.random.normal(key_seed, (FRAMES, PIX, WIDTH), jnp.float32), -4.0, 4.0)
    query_field = jnp.clip(jax.random.normal(query_seed, (FRAMES, PIX, WIDTH), jnp.float32), -4.0, 4.0)
    return (query_field, key_field)


def draw_queries(key, part):
    query_field, key_field = paired_fields(key)
    return query_field.astype(jnp.bfloat16)


def draw_key_rows(key, part):
    query_field, key_field = paired_fields(key)
    return key_field.astype(jnp.bfloat16)


def draw_tile_lists(key, part):
    side_seed = jax.random.fold_in(key, 23)
    sides = jax.random.randint(side_seed, (TILES,), 0, 2)
    own_tile = jnp.arange(TILES, dtype=jnp.int32)
    neighbour = (own_tile + 2 * sides - 1) % TILES
    return jnp.stack([own_tile, neighbour], axis=1).astype(jnp.int32)


def with_ends(drawn, rng, low, top_value):
    longest = drawn.shape.index(max(drawn.shape))
    spots = []
    for shift in (0, 1):
        where = [jax.random.randint(jax.random.fold_in(rng, axis), (), 0, length) for axis, length in enumerate(drawn.shape)]
        where[longest] = (where[longest] + shift) % drawn.shape[longest]
        spots.append(tuple(where))
    return drawn.at[spots[0]].set(low).at[spots[1]].set(top_value)


def block_scale(key, shape, pieces, smallest, top_value):
    def one(dim, parts):
        heights = jax.random.uniform(jax.random.fold_in(jax.random.fold_in(key, 6), dim), (parts,), jnp.float32, smallest / len(pieces), top_value / len(pieces))
        return jnp.repeat(jnp.exp(heights), shape[dim] // parts).reshape((-1,) + (1,) * (len(shape) - dim - 1))

    level = one(*pieces[0])
    for cut in pieces[1:]:
        level = level * one(*cut)
    return level


def centred(stream_key, shape, width, limit, cuts=(), kind=jnp.bfloat16):
    array = width * jax.random.normal(stream_key, shape, jnp.float32)
    if cuts:
        array = array * block_scale(stream_key, shape, cuts, -0.22, 0.18)
    return jnp.clip(array, -limit, limit).astype(kind)


def setup_inputs(seed: int = 0) -> dict:
    splits = jax.random.split(jax.random.key(seed), 6)
    return {
        "queries": draw_queries(jax.random.fold_in(splits[5], 71), 0),
        "key_rows": draw_key_rows(jax.random.fold_in(splits[5], 71), 0),
        "value_rows": centred(splits[2], (FRAMES, PIX, WIDTH), 1.0, 6.0, ((0, 4), (1, 64))),
        "dropout": with_ends((jax.random.randint(splits[3], (SAMPLES, FRAMES, PIX, HEADS), 0, 10) < 9).astype(jnp.int32), jax.random.fold_in(splits[3], 1), 0, 1),
        "tile_lists": draw_tile_lists(jax.random.fold_in(splits[5], 71), 0),
    }


keep_rate = 0.9

def head_reference(operands, allowed, factor):
    query_h, key_h, value_h, drop_h = operands
    scores = jnp.dot(query_h, key_h.T, preferred_element_type=jnp.float32) * factor
    masked = jnp.where(allowed, scores, -1e+30)
    highest = lax.optimization_barrier(jnp.max(masked, axis=1, keepdims=True))
    weight = jnp.exp(masked - highest)
    total = lax.optimization_barrier(jnp.sum(weight, axis=1))
    weight_low = lax.optimization_barrier(weight.astype(jnp.bfloat16))
    dropped = value_h.astype(jnp.float32)[None] * drop_h[:, :, None]
    summed = jnp.einsum('rk,skd->srd', weight_low.astype(jnp.float32), dropped)
    return (summed / (keep_rate * total)[None, :, None]).astype(jnp.bfloat16)

def reference(queries, key_rows, value_rows, dropout, tile_lists):
    factor = 1.0 / math.sqrt(HEAD_DIM)
    query_grid = queries.reshape(FRAMES, TILES, TILE_TOK, HEADS, HEAD_DIM)
    key_grid = key_rows.reshape(FRAMES, TILES, TILE_TOK, HEADS, HEAD_DIM)
    value_grid = value_rows.reshape(FRAMES, TILES, TILE_TOK, HEADS, HEAD_DIM)
    drop_grid = dropout.reshape(SAMPLES, FRAMES, TILES, TILE_TOK, HEADS).astype(jnp.float32)
    query_frame = jnp.repeat(jnp.arange(FRAMES, dtype=jnp.int32), TILE_TOK)
    key_frame = jnp.repeat(jnp.arange(FRAMES, dtype=jnp.int32), LIST_LEN * TILE_TOK)
    allowed = key_frame[None, :] <= query_frame[:, None]
    row_count = FRAMES * TILE_TOK
    key_total = FRAMES * LIST_LEN * TILE_TOK

    def one_tile(tile_id):
        chosen = tile_lists[tile_id]
        query_tile = query_grid[:, tile_id].reshape(row_count, HEADS, HEAD_DIM).transpose(1, 0, 2)
        key_tile = key_grid[:, chosen].reshape(key_total, HEADS, HEAD_DIM).transpose(1, 0, 2)
        value_tile = value_grid[:, chosen].reshape(key_total, HEADS, HEAD_DIM).transpose(1, 0, 2)
        drop_tile = drop_grid[:, :, chosen].reshape(SAMPLES, key_total, HEADS).transpose(2, 0, 1)
        result = lax.map(lambda operands: head_reference(operands, allowed, factor), (query_tile, key_tile, value_tile, drop_tile))
        return result.transpose(1, 2, 0, 3).reshape(SAMPLES, FRAMES, TILE_TOK, WIDTH)
    every_tile = lax.map(one_tile, jnp.arange(TILES, dtype=jnp.int32))
    return every_tile.transpose(1, 2, 0, 3, 4).reshape(SAMPLES, FRAMES, PIX, WIDTH)
```

```python
import functools
import math

import jax
import jax.numpy as jnp
from jax import lax
from jax.experimental import pallas as pl
from jax.experimental.pallas import tpu as pltpu
from jax.sharding import PartitionSpec as P

keep_rate = 0.9

F32 = jnp.float32
BF16 = jnp.bfloat16
SLOTS = (0, -1, 1, 2)


def shifted(x, axis, by):
    peers = lax.axis_size(axis)
    return lax.ppermute(x, axis, [(i, (i + by) % peers) for i in range(peers)])


def pack_body(place, *refs, chunk, per_dev, peers, rows, heads):
    drop_ref = refs[3 * peers]
    outs = refs[3 * peers + 1 :]
    me = place[0]
    drop = drop_ref[...].astype(F32).astype(BF16)
    head_id = lax.broadcasted_iota(jnp.int32, (8 * peers, heads), 1)
    row_id = lax.broadcasted_iota(jnp.int32, (8 * peers, heads), 0)
    wanted = lax.rem(me + row_id // 8, peers) * per_dev + chunk
    picker = jnp.where(head_id == wanted, 1.0, 0.0).astype(BF16)
    picked = lax.dot_general(
        picker, drop, (((1,), (1,)), ((), ())), preferred_element_type=F32
    )
    sub = lax.broadcasted_iota(jnp.int32, (8, 128), 0)
    for ahead in range(peers):
        q_ref, k_ref, v_ref = refs[3 * ahead : 3 * ahead + 3]
        out = outs[ahead]
        out[0:rows, :] = k_ref[...]
        out[rows : 2 * rows, :] = v_ref[...]
        mine = picked[8 * ahead : 8 * ahead + 8, :]
        bits = jnp.zeros((8, 128), F32)
        for r in range(8):
            bits = jnp.where(sub == r, mine[:, r * 128 : (r + 1) * 128], bits)
        both = jnp.concatenate([bits, jnp.zeros((8, 128), F32)], axis=0)
        out[2 * rows : 2 * rows + 16, :] = both.astype(BF16)
        out[2 * rows + 16 : 3 * rows + 16, :] = q_ref[...]


def pack(place, q, k, v, drop, chunk, per_dev, peers):
    rows, width = q.shape
    heads = drop.shape[1]
    dim = width // heads

    def column(ahead):
        return lambda i, place: (0, lax.rem(place[0] + ahead, peers) * per_dev + chunk)

    in_specs = []
    args = []
    for ahead in range(peers):
        for x in (q, k, v):
            in_specs.append(pl.BlockSpec((rows, dim), column(ahead)))
            args.append(x)
    in_specs.append(pl.BlockSpec(drop.shape, lambda i, place: (0, 0)))
    args.append(drop)
    size = 3 * rows + 16
    return pl.pallas_call(
        functools.partial(
            pack_body, chunk=chunk, per_dev=per_dev, peers=peers, rows=rows, heads=heads
        ),
        grid_spec=pltpu.PrefetchScalarGridSpec(
            num_scalar_prefetch=1,
            grid=(1,),
            in_specs=in_specs,
            out_specs=[pl.BlockSpec((size, dim), lambda i, place: (0, 0))] * peers,
        ),
        out_shape=[jax.ShapeDtypeStruct((size, dim), BF16)] * peers,
        cost_estimate=pl.CostEstimate(
            flops=0, bytes_accessed=2 * peers * size * dim * 2, transcendentals=0
        ),
        name="pack",
    )(place, *args)


def attend_body(place, *refs, rows, tok, samples, factor):
    slots = len(SLOTS)
    packs = refs[:slots]
    left, right = refs[slots : slots + 2]
    outs = refs[slots + 2 : 2 * slots + 2]
    keys, vals, score, acc = refs[2 * slots + 2 :]
    me = place[0]
    to_right = place[1] == 1
    dim = packs[0].shape[1]

    for i, off in enumerate(SLOTS):
        span = lax.rem(me + off + slots, slots)
        keys[span, 0:rows, :] = packs[i][0:rows, :]
        keys[span, rows : 2 * rows, :] = jnp.where(
            to_right, right[i, 0:rows, :], left[i, 0:rows, :]
        )
        for part in range(2):
            base = part * rows

            def take(a, b):
                if part == 0:
                    return packs[i][a:b, :]
                return jnp.where(to_right, right[i, a:b, :], left[i, a:b, :])

            bits = take(2 * rows, 2 * rows + 16).astype(F32)
            turned = bits[0:8, :].T
            halves = rows // 128
            for half in range(halves):
                value = take(rows + half * 128, rows + (half + 1) * 128)
                for s in range(samples):
                    r = s * halves + half
                    keep = jnp.broadcast_to(turned[:, r : r + 1], (128, dim))
                    vals[span, base + half * 128 : base + (half + 1) * 128, s * dim : (s + 1) * dim] = (
                        value * keep.astype(BF16)
                    )

    q_frame = lax.broadcasted_iota(jnp.int32, (rows, 2 * rows), 0) // tok
    k_frame = lax.rem(lax.broadcasted_iota(jnp.int32, (rows, 2 * rows), 1), rows) // tok
    frames = rows // tok
    lanes = 2 * rows // 128
    scale = factor * math.log2(math.e)

    for i, off in enumerate(SLOTS):
        span = lax.rem(me + off + slots, slots)
        q = packs[i][2 * rows + 16 : 3 * rows + 16, :]

        def first(j, top):
            s = lax.dot_general(
                q, keys[j], (((1,), (1,)), ((), ())), preferred_element_type=F32
            )
            s = jnp.where(k_frame <= q_frame + (span - j) * frames, s, -1e30)
            score[j] = s
            for b in range(lanes):
                top = jnp.maximum(top, s[:, b * 128 : (b + 1) * 128])
            return top

        top = lax.fori_loop(0, span + 1, first, jnp.full((rows, 128), -1e30, F32))
        top = jnp.max(top, axis=1, keepdims=True)
        acc[...] = jnp.zeros_like(acc)

        def second(j, total):
            w = jnp.exp2((score[j] - top) * scale)
            for b in range(lanes):
                total = total + w[:, b * 128 : (b + 1) * 128]
            acc[...] += jnp.dot(w.astype(BF16), vals[j], preferred_element_type=F32)
            return total

        total = lax.fori_loop(0, span + 1, second, jnp.zeros((rows, 128), F32))
        total = jnp.sum(total, axis=1, keepdims=True)
        inv = 1.0 / (keep_rate * total)
        for s in range(samples):
            outs[i][s] = (acc[:, s * dim : (s + 1) * dim] * inv).astype(BF16)


def attend(place, packs, left, right, rows, tok, samples):
    size, dim = packs[0].shape
    slots = len(SLOTS)
    piece = jax.ShapeDtypeStruct((samples, rows, dim), BF16)

    def whole(shape):
        return pl.BlockSpec(shape, lambda i, place: (0,) * len(shape))

    pairs = slots * (slots + 1) // 2
    return pl.pallas_call(
        functools.partial(
            attend_body, rows=rows, tok=tok, samples=samples, factor=1.0 / math.sqrt(dim)
        ),
        grid_spec=pltpu.PrefetchScalarGridSpec(
            num_scalar_prefetch=1,
            grid=(1,),
            in_specs=[whole(packs[0].shape)] * slots + [whole(left.shape)] * 2,
            out_specs=[whole(piece.shape)] * slots,
            scratch_shapes=[
                pltpu.VMEM((slots, 2 * rows, dim), BF16),
                pltpu.VMEM((slots, 2 * rows, samples * dim), BF16),
                pltpu.VMEM((slots, rows, 2 * rows), F32),
                pltpu.VMEM((rows, samples * dim), F32),
            ],
        ),
        out_shape=[piece] * slots,
        cost_estimate=pl.CostEstimate(
            flops=pairs * rows * 2 * rows * dim * 2 * (1 + samples),
            bytes_accessed=2 * slots * (size + 2 * left.shape[1] + samples * rows) * dim,
            transcendentals=pairs * rows * 2 * rows,
        ),
        name="attend",
    )(place, *packs, left, right)


def place_body(place, *refs, cols, dim, peers):
    pieces = refs[: len(cols)]
    out, sem = refs[-2:]
    copies = []
    for n, (back, mult, add) in enumerate(cols):
        col = lax.rem(place[0] + back, peers) * mult + add
        where = pl.ds(pl.multiple_of(col * dim, dim), dim)
        copies.append(pltpu.make_async_copy(pieces[n], out.at[:, :, where], sem.at[n]))
    for c in copies:
        c.start()
    for c in copies:
        c.wait()


def put(place, pieces, prior, shape, cols, peers):
    dim = pieces[0].shape[2]
    whole = pl.BlockSpec(pieces[0].shape, lambda i, place: (0, 0, 0))
    in_specs = [whole] * len(pieces)
    args = list(pieces)
    alias = {}
    if prior is not None:
        alias = {len(args) + 1: 0}
        in_specs.append(pl.BlockSpec(memory_space=pl.ANY))
        args.append(prior)
    return pl.pallas_call(
        functools.partial(place_body, cols=cols, dim=dim, peers=peers),
        grid_spec=pltpu.PrefetchScalarGridSpec(
            num_scalar_prefetch=1,
            grid=(1,),
            in_specs=in_specs,
            out_specs=pl.BlockSpec(memory_space=pl.ANY),
            scratch_shapes=[pltpu.SemaphoreType.DMA((len(pieces),))],
        ),
        out_shape=jax.ShapeDtypeStruct(shape, BF16),
        input_output_aliases=alias,
        cost_estimate=pl.CostEstimate(
            flops=0, bytes_accessed=4 * len(pieces) * pieces[0].size, transcendentals=0
        ),
        name="put",
    )(place, *args)


def per_device(queries, key_rows, value_rows, dropout, tile_lists):
    frame_dev, tok, width = queries.shape
    samples = dropout.shape[0]
    heads = dropout.shape[3]
    dim = width // heads
    rows = frame_dev * tok
    peers = lax.axis_size("tm")
    per_dev = heads // peers
    space = lax.axis_size("space")
    me = lax.axis_index("tm")
    tile = lax.axis_index("space")
    to_right = tile_lists[0, 1] == lax.rem(tile + 1, space)
    place = jnp.stack([me.astype(jnp.int32), to_right.astype(jnp.int32)])
    q = queries.reshape(rows, width)
    k = key_rows.reshape(rows, width)
    v = value_rows.reshape(rows, width)
    drop = dropout.reshape(samples * rows, heads)
    kept = 2 * rows + 16

    out = None
    for chunk in range(per_dev):
        own, next_, second_, prev_ = pack(place, q, k, v, drop, chunk, per_dev, peers)
        from_prev = shifted(next_, "tm", 1)
        from_next = shifted(prev_, "tm", -1)
        from_far = shifted(second_, "tm", 2)
        packs = (own, from_prev, from_next, from_far)
        column = jnp.stack([x[:kept] for x in packs])
        left = shifted(column, "space", 1)
        right = shifted(column, "space", -1)
        done = attend(place, packs, left, right, rows, tok, samples)
        came_next = shifted(done[1], "tm", -1)
        came_prev = shifted(done[2], "tm", 1)
        came_far = shifted(done[3], "tm", 2)
        cols = ((0, per_dev, chunk), (1, per_dev, chunk), (peers - 1, per_dev, chunk), (2, per_dev, chunk))
        out = put(
            place, (done[0], came_next, came_prev, came_far), out, (samples, rows, width), cols, peers
        )
    return out.reshape(samples, frame_dev, tok, width)


def solution(mesh):
    placed = (
        P("tm", "space", None),
        P("tm", "space", None),
        P("tm", "space", None),
        P(None, "tm", "space", None),
        P("space", None),
    )
    return jax.shard_map(
        per_device,
        mesh=mesh,
        in_specs=placed,
        out_specs=P(None, "tm", "space", None),
        check_vma=False,
    )
```

```python
import functools
import math

import jax
import jax.numpy as jnp
from jax import lax
from jax.experimental import pallas as pl
from jax.experimental.pallas import tpu as pltpu
from jax.sharding import PartitionSpec as P

keep_rate = 0.9

F32 = jnp.float32
BF16 = jnp.bfloat16
ANY = pl.BlockSpec(memory_space=pl.ANY)
BITS = 16


def paired(x, axis, mate):
    return lax.ppermute(x, axis, [(i, mate(i)) for i in range(lax.axis_size(axis))])


def pack_body(q, k, v, drop, *refs, peers, per_dev, chunk, rows, dim):
    outs = refs[:peers]
    buf, in_sem, out_sem = refs[peers:]
    me = lax.axis_index("tm")
    zero = jnp.zeros((BITS, dim - drop.shape[3]), BF16)
    loads = []
    for i in range(peers):
        head = (me ^ i) * per_dev + chunk
        where = pl.ds(pl.multiple_of(head * dim, dim), dim)
        group = []
        for n, (x, at) in enumerate(((k, 0), (v, rows), (q, 2 * rows + BITS))):
            group.append(
                pltpu.make_async_copy(x.at[:, where], buf.at[i, pl.ds(at, rows)], in_sem.at[i, n])
            )
        loads.append(group)
    order = (1, 2, 3, 0) if peers == 4 else range(peers)
    for i in order:
        for copy in loads[i]:
            copy.start()
    for i in range(peers):
        head = (me ^ i) * per_dev + chunk
        bits = drop[:, head].reshape(BITS, drop.shape[3])
        buf[i, 2 * rows : 2 * rows + BITS, :] = jnp.concatenate(
            [bits.astype(F32).astype(BF16), zero], axis=1
        )
    stores = [pltpu.make_async_copy(buf.at[i], outs[i], out_sem.at[i]) for i in range(peers)]
    for i in order:
        for copy in loads[i]:
            copy.wait()
        stores[i].start()
    for copy in stores:
        copy.wait()


def pack(q, k, v, drop, per_dev, peers, chunk):
    rows, width = q.shape
    dim = width // (per_dev * peers)
    size = 3 * rows + BITS
    return pl.pallas_call(
        functools.partial(
            pack_body, peers=peers, per_dev=per_dev, chunk=chunk, rows=rows, dim=dim
        ),
        in_specs=[ANY, ANY, ANY, pl.BlockSpec(memory_space=pltpu.VMEM)],
        out_specs=[ANY] * peers,
        scratch_shapes=[
            pltpu.VMEM((peers, size, dim), BF16),
            pltpu.SemaphoreType.DMA((peers, 3)),
            pltpu.SemaphoreType.DMA((peers,)),
        ],
        out_shape=[jax.ShapeDtypeStruct((size, dim), BF16)] * peers,
        cost_estimate=pl.CostEstimate(
            flops=0, bytes_accessed=4 * peers * size * dim, transcendentals=0
        ),
        name="pack",
    )(q, k, v, drop)


def attend_body(
    lists, *refs, slots, rows, tok, samples, factor
):
    packs = refs[:slots]
    near, far = refs[slots : slots + 2]
    outs = refs[slots + 2 : 2 * slots + 2]
    keys, vals, raw, bits, q_buf, done, in_sem, out_sem = refs[2 * slots + 2 :]
    dim = near.shape[2]
    frames = rows // tok
    me = lax.axis_index("tm")
    tile = lax.axis_index("space")
    use_near = lists[0, 1] == (tile ^ 1)

    def fetch(source, part, s):
        at = pl.multiple_of(2 * rows * s + part * rows, rows)
        return [
            pltpu.make_async_copy(source.at[pl.ds(0, rows)], keys.at[pl.ds(at, rows)], in_sem.at[s, 3 * part]),
            pltpu.make_async_copy(source.at[pl.ds(rows, rows)], raw.at[s, part], in_sem.at[s, 3 * part + 1]),
            pltpu.make_async_copy(source.at[pl.ds(2 * rows, BITS)], bits.at[s, part], in_sem.at[s, 3 * part + 2]),
        ]

    def fetch_q(i, s):
        return pltpu.make_async_copy(
            packs[i].at[pl.ds(2 * rows + BITS, rows)], q_buf.at[s], in_sem.at[s, 6]
        )

    for i in range(slots):
        s = me ^ i
        for copy in fetch(packs[i], 0, s):
            copy.start()
        fetch_q(i, s).start()

    @pl.when(use_near)
    def _():
        for i in range(slots):
            for copy in fetch(near.at[i], 1, me ^ i):
                copy.start()

    @pl.when(jnp.logical_not(use_near))
    def _():
        for i in range(slots):
            for copy in fetch(far.at[i], 1, me ^ i):
                copy.start()

    for s in range(slots):
        for copy in fetch(packs[0], 0, s) + fetch(near.at[0], 1, s):
            copy.wait()
        fetch_q(0, s).wait()

    q_frame = lax.broadcasted_iota(jnp.int32, (rows, 2 * rows), 0) // tok
    k_frame = lax.rem(lax.broadcasted_iota(jnp.int32, (rows, 2 * rows), 1), rows) // tok
    causal = k_frame <= q_frame
    scale = factor * math.log2(math.e)

    def get_scores(s):
        cols = 2 * rows * (s + 1)
        score = lax.dot_general(
            q_buf[s], keys[0:cols, :], (((1,), (1,)), ((), ())), preferred_element_type=F32
        )
        last = jnp.where(causal, score[:, 2 * rows * s :], -1e30)
        return jnp.concatenate([score[:, : 2 * rows * s], last], axis=1) if s else last

    def stage(s):
        for part in range(2):
            turned = bits[s, part].T
            for f in range(frames):
                value = raw[s, part, f * tok : (f + 1) * tok, :]
                at = 2 * rows * s + part * rows + f * tok
                for n in range(samples):
                    r = n * frames + f
                    keep = jnp.broadcast_to(turned[0:tok, r : r + 1], (tok, dim))
                    vals[at : at + tok, n * dim : (n + 1) * dim] = value * keep

    score = get_scores(0)
    for s in range(slots):
        ahead = get_scores(s + 1) if s + 1 < slots else None
        stage(s)
        cols = 2 * rows * (s + 1)
        top = jnp.max(score, axis=1, keepdims=True)
        w = jnp.exp2((score - top) * scale)
        total = jnp.sum(w, axis=1, keepdims=True)
        acc = jnp.dot(w.astype(BF16), vals[0:cols, :], preferred_element_type=F32)
        inv = 1.0 / (keep_rate * total)
        for n in range(samples):
            done[s, n] = (acc[:, n * dim : (n + 1) * dim] * inv).astype(BF16)
        score = ahead
    sends = [pltpu.make_async_copy(done.at[me ^ i], outs[i], out_sem.at[i]) for i in range(slots)]
    for copy in sends:
        copy.start()
    for copy in sends:
        copy.wait()


def attend(lists, packs, near, far, rows, tok, samples):
    size, dim = packs[0].shape
    slots = len(packs)
    pairs = slots * (slots + 1) // 2
    return pl.pallas_call(
        functools.partial(
            attend_body, slots=slots, rows=rows, tok=tok, samples=samples, factor=1.0 / math.sqrt(dim)
        ),
        in_specs=[pl.BlockSpec(memory_space=pltpu.SMEM)] + [ANY] * (slots + 2),
        out_specs=[ANY] * slots,
        scratch_shapes=[
            pltpu.VMEM((slots * 2 * rows, dim), BF16),
            pltpu.VMEM((slots * 2 * rows, samples * dim), BF16),
            pltpu.VMEM((slots, 2, rows, dim), BF16),
            pltpu.VMEM((slots, 2, BITS, dim), BF16),
            pltpu.VMEM((slots, rows, dim), BF16),
            pltpu.VMEM((slots, samples, rows, dim), BF16),
            pltpu.SemaphoreType.DMA((slots, 7)),
            pltpu.SemaphoreType.DMA((slots,)),
        ],
        out_shape=[jax.ShapeDtypeStruct((samples, rows, dim), BF16)] * slots,
        cost_estimate=pl.CostEstimate(
            flops=pairs * rows * 2 * rows * dim * 2 * (1 + samples),
            bytes_accessed=2 * slots * (2 * size + samples * rows) * dim,
            transcendentals=pairs * rows * 2 * rows,
        ),
        name="attend",
    )(lists, *packs, near, far)


def put_body(*refs, peers, per_dev, chunk, dim):
    pieces = refs[:peers]
    out, buf, in_sem, out_sem = refs[-4:]
    me = lax.axis_index("tm")
    loads = []
    stores = []
    for i in range(peers):
        where = pl.ds(pl.multiple_of(((me ^ i) * per_dev + chunk) * dim, dim), dim)
        loads.append(pltpu.make_async_copy(pieces[i], buf.at[i], in_sem.at[i]))
        stores.append(pltpu.make_async_copy(buf.at[i], out.at[:, :, where], out_sem.at[i]))
    for copy in loads:
        copy.start()
    for load, store in zip(loads, stores):
        load.wait()
        store.start()
    for copy in stores:
        copy.wait()


def put(pieces, prior, shape, per_dev, chunk):
    peers = len(pieces)
    samples, rows, dim = pieces[0].shape
    args = list(pieces) if prior is None else list(pieces) + [prior]
    return pl.pallas_call(
        functools.partial(put_body, peers=peers, per_dev=per_dev, chunk=chunk, dim=dim),
        in_specs=[ANY] * len(args),
        out_specs=ANY,
        scratch_shapes=[
            pltpu.VMEM((peers,) + pieces[0].shape, BF16),
            pltpu.SemaphoreType.DMA((peers,)),
            pltpu.SemaphoreType.DMA((peers,)),
        ],
        out_shape=jax.ShapeDtypeStruct(shape, BF16),
        input_output_aliases={} if prior is None else {peers: 0},
        cost_estimate=pl.CostEstimate(
            flops=0, bytes_accessed=4 * peers * pieces[0].size, transcendentals=0
        ),
        name="put",
    )(*args)


def per_device(queries, key_rows, value_rows, dropout, tile_lists):
    frame_dev, tok, width = queries.shape
    samples = dropout.shape[0]
    heads = dropout.shape[3]
    rows = frame_dev * tok
    peers = lax.axis_size("tm")
    per_dev = heads // peers
    space = lax.axis_size("space")
    q = queries.reshape(rows, width)
    k = key_rows.reshape(rows, width)
    v = value_rows.reshape(rows, width)
    drop = dropout.transpose(0, 3, 1, 2)
    kept = 2 * rows + BITS

    def swap(x, i):
        return paired(x, "tm", lambda n: n ^ i)

    out = None
    for chunk in range(per_dev):
        own, *away = pack(q, k, v, drop, per_dev, peers, chunk)
        packs = [own] + [swap(x, i + 1) for i, x in enumerate(away)]
        column = jnp.stack([x[:kept] for x in packs])
        near = paired(column, "space", lambda n: n ^ 1)
        far = paired(column, "space", lambda n: (((n + 1) ^ 1) - 1) % space)
        done = attend(tile_lists, packs, near, far, rows, tok, samples)
        pieces = [done[0]] + [swap(x, i + 1) for i, x in enumerate(done[1:])]
        out = put(pieces, out, (samples, rows, width), per_dev, chunk)
    return out.reshape(samples, frame_dev, tok, width)


def solution(mesh):
    placed = (
        P("tm", "space", None),
        P("tm", "space", None),
        P("tm", "space", None),
        P(None, "tm", "space", None),
        P("space", None),
    )
    return jax.shard_map(
        per_device,
        mesh=mesh,
        in_specs=placed,
        out_specs=P(None, "tm", "space", None),
        check_vma=False,
    )
```

```python
import functools
import math

import jax
import jax.numpy as jnp
from jax import lax
from jax.experimental import pallas as pl
from jax.experimental.pallas import tpu as pltpu
from jax.sharding import PartitionSpec as P

keep_rate = 0.9

F32 = jnp.float32
BF16 = jnp.bfloat16
ANY = pl.BlockSpec(memory_space=pl.ANY)
HBM = pl.BlockSpec(memory_space=pltpu.HBM)
BITS = 16
LIMIT = 12 << 20
PACK_LIMIT = 60 << 20


def paired(x, axis, mate):
    return lax.ppermute(x, axis, [(i, mate(i)) for i in range(lax.axis_size(axis))])


def layout(package, rows):
    at = 2 * rows + BITS
    return at + rows * len(package[1])


def pack_body(q, k, v, drop, *refs, peers, per_dev, packages, rows, dim):
    outs = refs[: peers * len(packages)]
    in_sem = refs[-1]
    me = lax.axis_index("tm")
    zero = jnp.zeros((BITS, dim - drop.shape[3]), BF16)
    plan = [(n, i) for n in range(len(packages)) for i in tuple(range(1, peers)) + (0,)]
    loads = []
    for n, i in plan:
        chunk, asked = packages[n]
        out = outs[n * peers + i]
        parts = [(k, chunk, 0), (v, chunk, rows)]
        parts += [(q, c, (2 + m) * rows + BITS) for m, c in enumerate(asked)]
        for m, (x, c, at) in enumerate(parts):
            where = pl.ds(pl.multiple_of(((me ^ i) * per_dev + c) * dim, dim), dim)
            loads.append(
                pltpu.make_async_copy(x.at[:, where], out.at[pl.ds(at, rows)], in_sem.at[n, i, m])
            )
            loads[-1].start()
    for n, i in plan:
        bits = drop[:, (me ^ i) * per_dev + packages[n][0]].reshape(BITS, drop.shape[3])
        outs[n * peers + i][2 * rows : 2 * rows + BITS, :] = jnp.concatenate(
            [bits.astype(F32).astype(BF16), zero], axis=1
        )
    for copy in loads:
        copy.wait()


def pack(q, k, v, drop, per_dev, peers, packages):
    rows, width = q.shape
    dim = width // (per_dev * peers)
    sizes = [layout(package, rows) for package in packages for _ in range(peers)]
    flat = pl.pallas_call(
        functools.partial(
            pack_body, peers=peers, per_dev=per_dev, packages=packages, rows=rows, dim=dim
        ),
        in_specs=[HBM, HBM, HBM, pl.BlockSpec(memory_space=pltpu.VMEM)],
        out_specs=[pl.BlockSpec(memory_space=pltpu.VMEM)] * len(sizes),
        scratch_shapes=[
            pltpu.SemaphoreType.DMA((len(packages), peers, 2 + max(len(p[1]) for p in packages)))
        ],
        out_shape=[pltpu.VMEM((size, dim), BF16) for size in sizes],
        compiler_params=pltpu.CompilerParams(vmem_limit_bytes=PACK_LIMIT),
        cost_estimate=pl.CostEstimate(
            flops=0, bytes_accessed=4 * sum(sizes) * dim, transcendentals=0
        ),
        name="pack",
    )(q, k, v, drop)
    return [flat[n * peers : (n + 1) * peers] for n in range(len(packages))]


def attend_body(
    lists, column, near, far, *refs, slots, ask_at, rows, tok, samples, factor
):
    asks = refs[:slots]
    outs = refs[slots : 2 * slots]
    keys, vals, q_buf, done, out_sem = refs[2 * slots :]
    dim = near.shape[2]
    half = rows // 2
    span_keys = 2 * rows
    me = lax.axis_index("tm")
    use_near = lists[0, 1] == (lax.axis_index("space") ^ 1)

    for i in range(slots):
        q_buf[me ^ i] = asks[i][ask_at : ask_at + rows, :]

    def part(s, side, at, size):
        slot = me ^ s
        if side == 0:
            return column[slot, at : at + size, :]
        return jnp.where(use_near, near[slot, at : at + size, :], far[slot, at : at + size, :])

    def stage_keys(s):
        for late in range(2):
            for side in range(2):
                at = s * span_keys + (2 * late + side) * half
                keys[at : at + half, :] = part(s, side, late * half, half)

    def stage_values(s):
        for side in range(2):
            turned = part(s, side, 2 * rows, BITS).T
            for f in range(rows // tok):
                value = part(s, side, rows + f * tok, tok)
                late, rest = divmod(f * tok, half)
                at = s * span_keys + (2 * late + side) * half + rest
                for n in range(samples):
                    r = n * (rows // tok) + f
                    keep = jnp.broadcast_to(turned[0:tok, r : r + 1], (tok, dim))
                    vals[at : at + tok, n * dim : (n + 1) * dim] = value * keep

    row_frame = lax.broadcasted_iota(jnp.int32, (rows, rows), 0) // tok
    key_frame = lax.rem(lax.broadcasted_iota(jnp.int32, (rows, rows), 1), half) // tok
    early = key_frame <= row_frame
    late = (key_frame <= row_frame)[:half]
    scale = factor * math.log2(math.e)

    def dot_keys(q, lo, hi):
        return lax.dot_general(
            q, keys[lo:hi, :], (((1,), (1,)), ((), ())), preferred_element_type=F32
        )

    def get_scores(s):
        base = s * span_keys
        q = q_buf[s]
        wide = dot_keys(q, 0, base + rows)
        last = jnp.where(early, wide[:, base:], -1e30)
        wide = jnp.concatenate([wide[:, :base], last], axis=1) if s else last
        tail = jnp.where(late, dot_keys(q[half:], base + rows, base + span_keys), -1e30)
        return wide, tail

    def finish(s, wide, tail):
        base = s * span_keys
        top = jnp.max(wide, axis=1, keepdims=True)
        low_top = jnp.maximum(top[half:], jnp.max(tail, axis=1, keepdims=True))
        top = jnp.concatenate([top[:half], low_top], axis=0)
        w = jnp.exp2((wide - top) * scale)
        w_tail = jnp.exp2((tail - low_top) * scale)
        total = jnp.sum(w, axis=1, keepdims=True)
        low_total = total[half:] + jnp.sum(w_tail, axis=1, keepdims=True)
        acc = jnp.dot(w.astype(BF16), vals[0 : base + rows, :], preferred_element_type=F32)
        more = jnp.dot(
            w_tail.astype(BF16),
            vals[base + rows : base + span_keys, :],
            preferred_element_type=F32,
        )
        for lo, acc_part, sum_part in (
            (0, acc[:half], total[:half]),
            (half, acc[half:] + more, low_total),
        ):
            inv = 1.0 / (keep_rate * sum_part)
            for n in range(samples):
                done[s, n, lo : lo + half, :] = (
                    acc_part[:, n * dim : (n + 1) * dim] * inv
                ).astype(BF16)

    stage_keys(0)
    scores = get_scores(0)
    for s in range(slots):
        if s + 1 < slots:
            stage_keys(s + 1)
            ahead = get_scores(s + 1)
        stage_values(s)
        finish(s, *scores)
        scores = ahead
    sends = [pltpu.make_async_copy(done.at[me ^ i], outs[i], out_sem.at[i]) for i in range(slots)]
    for copy in sends:
        copy.start()
    for copy in sends:
        copy.wait()


def attend(lists, column, near, far, asks, ask_at, rows, tok, samples):
    slots, size, dim = column.shape
    pairs = slots * (slots + 1) // 2
    inside = pl.BlockSpec(memory_space=pltpu.VMEM)
    return pl.pallas_call(
        functools.partial(
            attend_body,
            slots=slots,
            ask_at=ask_at,
            rows=rows,
            tok=tok,
            samples=samples,
            factor=1.0 / math.sqrt(dim),
        ),
        in_specs=[pl.BlockSpec(memory_space=pltpu.SMEM)] + [inside] * (slots + 3),
        out_specs=[ANY] * slots,
        scratch_shapes=[
            pltpu.VMEM((slots * 2 * rows, dim), BF16),
            pltpu.VMEM((slots * 2 * rows, samples * dim), BF16),
            pltpu.VMEM((slots, rows, dim), BF16),
            pltpu.VMEM((slots, samples, rows, dim), BF16),
            pltpu.SemaphoreType.DMA((slots,)),
        ],
        out_shape=[jax.ShapeDtypeStruct((samples, rows, dim), BF16)] * slots,
        compiler_params=pltpu.CompilerParams(vmem_limit_bytes=LIMIT),
        cost_estimate=pl.CostEstimate(
            flops=pairs * rows * 2 * rows * dim * 2 * (1 + samples),
            bytes_accessed=2 * slots * (2 * size + samples * rows) * dim,
            transcendentals=pairs * rows * 2 * rows,
        ),
        name="attend",
    )(lists, column, near, far, *asks)


def put_body(*refs, peers, per_dev, chunk, dim):
    pieces = refs[:peers]
    out, buf, in_sem, out_sem = refs[-4:]
    me = lax.axis_index("tm")
    loads = []
    stores = []
    for i in range(peers):
        where = pl.ds(pl.multiple_of(((me ^ i) * per_dev + chunk) * dim, dim), dim)
        loads.append(pltpu.make_async_copy(pieces[i], buf.at[i], in_sem.at[i]))
        stores.append(pltpu.make_async_copy(buf.at[i], out.at[:, :, where], out_sem.at[i]))
    for copy in loads:
        copy.start()
    for load, store in zip(loads, stores):
        load.wait()
        store.start()
    for copy in stores:
        copy.wait()


def put(pieces, prior, shape, per_dev, chunk):
    peers = len(pieces)
    _, _, dim = pieces[0].shape
    args = list(pieces) if prior is None else list(pieces) + [prior]
    return pl.pallas_call(
        functools.partial(put_body, peers=peers, per_dev=per_dev, chunk=chunk, dim=dim),
        in_specs=[ANY] * len(args),
        out_specs=ANY,
        scratch_shapes=[
            pltpu.VMEM((peers,) + pieces[0].shape, BF16),
            pltpu.SemaphoreType.DMA((peers,)),
            pltpu.SemaphoreType.DMA((peers,)),
        ],
        out_shape=jax.ShapeDtypeStruct(shape, BF16),
        input_output_aliases={} if prior is None else {peers: 0},
        compiler_params=pltpu.CompilerParams(vmem_limit_bytes=LIMIT),
        cost_estimate=pl.CostEstimate(
            flops=0, bytes_accessed=4 * peers * pieces[0].size, transcendentals=0
        ),
        name="put",
    )(*args)


def per_device(queries, key_rows, value_rows, dropout, tile_lists):
    frame_dev, tok, width = queries.shape
    samples = dropout.shape[0]
    heads = dropout.shape[3]
    rows = frame_dev * tok
    peers = lax.axis_size("tm")
    per_dev = heads // peers
    space = lax.axis_size("space")
    q = queries.reshape(rows, width)
    k = key_rows.reshape(rows, width)
    v = value_rows.reshape(rows, width)
    drop = dropout.transpose(0, 3, 1, 2)
    kept = 2 * rows + BITS

    shape = (samples, rows, width)

    def spread(group):
        moved = [group[0]]
        for i in range(1, peers):
            moved.append(paired(group[i], "tm", lambda n: n ^ i))
        return moved

    def widen(packs):
        column = jnp.stack([x[:kept] for x in packs])
        near = paired(column, "space", lambda n: n ^ 1)
        far = paired(column, "space", lambda n: (((n + 1) ^ 1) - 1) % space)
        return column, near, far

    out = None
    groups = pack(q, k, v, drop, per_dev, peers, PACKAGES[:1])
    groups += pack(q, k, v, drop, per_dev, peers, PACKAGES[1:])
    packs = [spread(groups[n]) for n in range(per_dev)]
    results = []
    for chunk in range(per_dev):
        sides = widen(packs[chunk])
        source = [n for n in range(per_dev) if chunk in PACKAGES[n][1]][0]
        ask_at = kept + rows * PACKAGES[source][1].index(chunk)
        done = attend(tile_lists, *sides, packs[source], ask_at, rows, tok, samples)
        results.append(spread(done))
    for chunk in range(per_dev):
        out = put(results[chunk], out, shape, per_dev, chunk)
    return out.reshape(samples, frame_dev, tok, width)


PACKAGES = ((0, (0,)), (1, (1,)), (2, (2,)))


def solution(mesh):
    placed = (
        P("tm", "space", None),
        P("tm", "space", None),
        P("tm", "space", None),
        P(None, "tm", "space", None),
        P("space", None),
    )
    return jax.shard_map(
        per_device,
        mesh=mesh,
        in_specs=placed,
        out_specs=P(None, "tm", "space", None),
        check_vma=False,
    )
```

```python
import functools
import math

import jax
import jax.numpy as jnp
from jax import lax
from jax.experimental import pallas as pl
from jax.experimental.pallas import tpu as pltpu
from jax.sharding import PartitionSpec as P

keep_rate = 0.9

F32 = jnp.float32
BF16 = jnp.bfloat16
ANY = pl.BlockSpec(memory_space=pl.ANY)
HBM = pl.BlockSpec(memory_space=pltpu.HBM)
BITS = 16
LIMIT = 12 << 20
PACK_LIMIT = 60 << 20


def paired(x, axis, mate):
    return lax.ppermute(x, axis, [(i, mate(i)) for i in range(lax.axis_size(axis))])


def layout(package, rows):
    at = 2 * rows + BITS
    return at + rows * len(package[1])


def pack_body(q, k, v, drop, *refs, peers, per_dev, packages, rows, dim):
    outs = refs[: peers * len(packages)]
    flags, in_sem, flag_sem = refs[peers * len(packages) :]
    me = lax.axis_index("tm")
    zero = jnp.zeros((BITS, dim - drop.shape[3]), BF16)
    plan = [(n, i) for n in range(len(packages)) for i in tuple(range(1, peers)) + (0,)]
    loads = []
    for n, i in plan:
        chunk, asked = packages[n]
        out = outs[n * peers + i]
        parts = [(k, chunk, 0), (v, chunk, rows)]
        parts += [(q, c, (2 + m) * rows + BITS) for m, c in enumerate(asked)]
        for m, (x, c, at) in enumerate(parts):
            where = pl.ds(pl.multiple_of(((me ^ i) * per_dev + c) * dim, dim), dim)
            loads.append(
                pltpu.make_async_copy(x.at[:, where], out.at[pl.ds(at, rows)], in_sem.at[n, i, m])
            )
            loads[-1].start()
    flag_loads = {}
    for n, i in plan:
        head = (me ^ i) * per_dev + packages[n][0]
        flag_loads[n, i] = pltpu.make_async_copy(drop.at[:, head], flags.at[n, i], flag_sem.at[n, i])
        flag_loads[n, i].start()
    for n, i in plan:
        flag_loads[n, i].wait()
        bits = flags[n, i].reshape(BITS, drop.shape[3])
        outs[n * peers + i][2 * rows : 2 * rows + BITS, :] = jnp.concatenate(
            [bits.astype(F32).astype(BF16), zero], axis=1
        )
    for copy in loads:
        copy.wait()


def pack(q, k, v, drop, per_dev, peers, packages):
    rows, width = q.shape
    dim = width // (per_dev * peers)
    sizes = [layout(package, rows) for package in packages for _ in range(peers)]
    flat = pl.pallas_call(
        functools.partial(
            pack_body, peers=peers, per_dev=per_dev, packages=packages, rows=rows, dim=dim
        ),
        in_specs=[HBM] * 4,
        out_specs=[pl.BlockSpec(memory_space=pltpu.VMEM)] * len(sizes),
        scratch_shapes=[
            pltpu.VMEM((len(packages), peers, drop.shape[0]) + drop.shape[2:], drop.dtype),
            pltpu.SemaphoreType.DMA((len(packages), peers, 2 + max(len(p[1]) for p in packages))),
            pltpu.SemaphoreType.DMA((len(packages), peers)),
        ],
        out_shape=[pltpu.VMEM((size, dim), BF16) for size in sizes],
        compiler_params=pltpu.CompilerParams(vmem_limit_bytes=PACK_LIMIT),
        cost_estimate=pl.CostEstimate(
            flops=0, bytes_accessed=4 * sum(sizes) * dim, transcendentals=0
        ),
        name="pack",
    )(q, k, v, drop)
    return [flat[n * peers : (n + 1) * peers] for n in range(len(packages))]


def attend_body(
    lists, column, near, far, *refs, slots, ask_at, rows, tok, samples, factor
):
    asks = refs[:slots]
    outs = refs[slots : 2 * slots]
    keys, vals, q_buf, done, out_sem = refs[2 * slots :]
    dim = near.shape[2]
    half = rows // 2
    span_keys = 2 * rows
    me = lax.axis_index("tm")
    use_near = lists[0, 1] == (lax.axis_index("space") ^ 1)

    for i in range(slots):
        q_buf[me ^ i] = asks[i][ask_at : ask_at + rows, :]

    def part(s, side, at, size):
        slot = me ^ s
        if side == 0:
            return column[slot, at : at + size, :]
        return jnp.where(use_near, near[slot, at : at + size, :], far[slot, at : at + size, :])

    def stage_keys(s):
        for late in range(2):
            for side in range(2):
                at = s * span_keys + (2 * late + side) * half
                keys[at : at + half, :] = part(s, side, late * half, half)

    def stage_values(s):
        for side in range(2):
            turned = part(s, side, 2 * rows, BITS).T
            for f in range(rows // tok):
                value = part(s, side, rows + f * tok, tok)
                late, rest = divmod(f * tok, half)
                at = s * span_keys + (2 * late + side) * half + rest
                for n in range(samples):
                    r = n * (rows // tok) + f
                    keep = jnp.broadcast_to(turned[0:tok, r : r + 1], (tok, dim))
                    vals[at : at + tok, n * dim : (n + 1) * dim] = value * keep

    row_frame = lax.broadcasted_iota(jnp.int32, (rows, rows), 0) // tok
    key_frame = lax.rem(lax.broadcasted_iota(jnp.int32, (rows, rows), 1), half) // tok
    early = key_frame <= row_frame
    late = (key_frame <= row_frame)[:half]
    scale = factor * math.log2(math.e)

    def dot_keys(q, lo, hi):
        return lax.dot_general(
            q, keys[lo:hi, :], (((1,), (1,)), ((), ())), preferred_element_type=F32
        )

    def get_scores(s):
        base = s * span_keys
        q = q_buf[s]
        wide = dot_keys(q, 0, base + rows)
        last = jnp.where(early, wide[:, base:], -1e30)
        wide = jnp.concatenate([wide[:, :base], last], axis=1) if s else last
        tail = jnp.where(late, dot_keys(q[half:], base + rows, base + span_keys), -1e30)
        return wide, tail

    def finish(s, wide, tail):
        base = s * span_keys
        top = jnp.max(wide, axis=1, keepdims=True)
        low_top = jnp.maximum(top[half:], jnp.max(tail, axis=1, keepdims=True))
        top = jnp.concatenate([top[:half], low_top], axis=0)
        w = jnp.exp2((wide - top) * scale)
        w_tail = jnp.exp2((tail - low_top) * scale)
        total = jnp.sum(w, axis=1, keepdims=True)
        low_total = total[half:] + jnp.sum(w_tail, axis=1, keepdims=True)
        acc = jnp.dot(w.astype(BF16), vals[0 : base + rows, :], preferred_element_type=F32)
        more = jnp.dot(
            w_tail.astype(BF16),
            vals[base + rows : base + span_keys, :],
            preferred_element_type=F32,
        )
        for lo, acc_part, sum_part in (
            (0, acc[:half], total[:half]),
            (half, acc[half:] + more, low_total),
        ):
            inv = 1.0 / (keep_rate * sum_part)
            for n in range(samples):
                done[s, n, lo : lo + half, :] = (
                    acc_part[:, n * dim : (n + 1) * dim] * inv
                ).astype(BF16)

    stage_keys(0)
    scores = get_scores(0)
    for s in range(slots):
        if s + 1 < slots:
            stage_keys(s + 1)
            ahead = get_scores(s + 1)
        stage_values(s)
        finish(s, *scores)
        scores = ahead
    sends = [pltpu.make_async_copy(done.at[me ^ i], outs[i], out_sem.at[i]) for i in range(slots)]
    for copy in sends:
        copy.start()
    for copy in sends:
        copy.wait()


def attend(lists, column, near, far, asks, ask_at, rows, tok, samples):
    slots, size, dim = column.shape
    pairs = slots * (slots + 1) // 2
    inside = pl.BlockSpec(memory_space=pltpu.VMEM)
    return pl.pallas_call(
        functools.partial(
            attend_body,
            slots=slots,
            ask_at=ask_at,
            rows=rows,
            tok=tok,
            samples=samples,
            factor=1.0 / math.sqrt(dim),
        ),
        in_specs=[pl.BlockSpec(memory_space=pltpu.SMEM)] + [inside] * (slots + 3),
        out_specs=[ANY] * slots,
        scratch_shapes=[
            pltpu.VMEM((slots * 2 * rows, dim), BF16),
            pltpu.VMEM((slots * 2 * rows, samples * dim), BF16),
            pltpu.VMEM((slots, rows, dim), BF16),
            pltpu.VMEM((slots, samples, rows, dim), BF16),
            pltpu.SemaphoreType.DMA((slots,)),
        ],
        out_shape=[jax.ShapeDtypeStruct((samples, rows, dim), BF16)] * slots,
        compiler_params=pltpu.CompilerParams(vmem_limit_bytes=LIMIT),
        cost_estimate=pl.CostEstimate(
            flops=pairs * rows * 2 * rows * dim * 2 * (1 + samples),
            bytes_accessed=2 * slots * (2 * size + samples * rows) * dim,
            transcendentals=pairs * rows * 2 * rows,
        ),
        name="attend",
    )(lists, column, near, far, *asks)


def put_body(*refs, slots, per_dev, chunk, dim):
    pieces = refs[: len(slots)]
    out, buf, in_sem, out_sem = refs[-4:]
    me = lax.axis_index("tm")
    loads = []
    stores = []
    for n, i in enumerate(slots):
        where = pl.ds(pl.multiple_of(((me ^ i) * per_dev + chunk) * dim, dim), dim)
        loads.append(pltpu.make_async_copy(pieces[n], buf.at[n], in_sem.at[n]))
        stores.append(pltpu.make_async_copy(buf.at[n], out.at[:, :, where], out_sem.at[n]))
    for copy in loads:
        copy.start()
    for load, store in zip(loads, stores):
        load.wait()
        store.start()
    for copy in stores:
        copy.wait()


def put(pieces, slots, prior, shape, per_dev, chunk):
    pieces = [pieces[i] for i in slots]
    peers = len(pieces)
    _, _, dim = pieces[0].shape
    args = list(pieces) if prior is None else list(pieces) + [prior]
    return pl.pallas_call(
        functools.partial(put_body, slots=slots, per_dev=per_dev, chunk=chunk, dim=dim),
        in_specs=[ANY] * len(args),
        out_specs=ANY,
        scratch_shapes=[
            pltpu.VMEM((peers,) + pieces[0].shape, BF16),
            pltpu.SemaphoreType.DMA((peers,)),
            pltpu.SemaphoreType.DMA((peers,)),
        ],
        out_shape=jax.ShapeDtypeStruct(shape, BF16),
        input_output_aliases={} if prior is None else {peers: 0},
        compiler_params=pltpu.CompilerParams(vmem_limit_bytes=LIMIT),
        cost_estimate=pl.CostEstimate(
            flops=0, bytes_accessed=4 * peers * pieces[0].size, transcendentals=0
        ),
        name="put",
    )(*args)


def per_device(queries, key_rows, value_rows, dropout, tile_lists):
    frame_dev, tok, width = queries.shape
    samples = dropout.shape[0]
    heads = dropout.shape[3]
    rows = frame_dev * tok
    peers = lax.axis_size("tm")
    per_dev = heads // peers
    space = lax.axis_size("space")
    q = queries.reshape(rows, width)
    k = key_rows.reshape(rows, width)
    v = value_rows.reshape(rows, width)
    drop = dropout.transpose(0, 3, 1, 2)
    kept = 2 * rows + BITS

    shape = (samples, rows, width)

    def spread(group):
        moved = [group[0]]
        for i in range(1, peers):
            moved.append(paired(group[i], "tm", lambda n: n ^ i))
        return moved

    def widen(packs):
        column = jnp.stack([x[:kept] for x in packs])
        near = paired(column, "space", lambda n: n ^ 1)
        far = paired(column, "space", lambda n: (((n + 1) ^ 1) - 1) % space)
        return column, near, far

    out = None
    groups = pack(q, k, v, drop, per_dev, peers, PACKAGES[:1])
    groups += pack(q, k, v, drop, per_dev, peers, PACKAGES[1:])
    packs = [spread(groups[n]) for n in range(per_dev)]
    results = []
    for chunk in range(per_dev):
        sides = widen(packs[chunk])
        source = [n for n in range(per_dev) if chunk in PACKAGES[n][1]][0]
        ask_at = kept + rows * PACKAGES[source][1].index(chunk)
        done = attend(tile_lists, *sides, packs[source], ask_at, rows, tok, samples)
        results.append(spread(done))
    for chunk, slots in PUTS:
        out = put(results[chunk], slots, out, shape, per_dev, chunk)
    return out.reshape(samples, frame_dev, tok, width)


PACKAGES = ((0, ()), (1, (0,)), (2, (1, 2)))


PUTS = ((0, (0, 1, 2, 3)), (1, (0, 1, 2, 3)), (2, (0, 1)), (2, (3, 2)))


def solution(mesh):
    placed = (
        P("tm", "space", None),
        P("tm", "space", None),
        P("tm", "space", None),
        P(None, "tm", "space", None),
        P("space", None),
    )
    return jax.shard_map(
        per_device,
        mesh=mesh,
        in_specs=placed,
        out_specs=P(None, "tm", "space", None),
        check_vma=False,
    )
```

```python
import functools
import math

import jax
import jax.numpy as jnp
from jax import lax
from jax.experimental import pallas as pl
from jax.experimental.pallas import tpu as pltpu
from jax.sharding import PartitionSpec as P

keep_rate = 0.9

F32 = jnp.float32
BF16 = jnp.bfloat16
ANY = pl.BlockSpec(memory_space=pl.ANY)
HBM = pl.BlockSpec(memory_space=pltpu.HBM)
BITS = 16
LIMIT = 12 << 20
PACK_LIMIT = 60 << 20


def paired(x, axis, mate):
    return lax.ppermute(x, axis, [(i, mate(i)) for i in range(lax.axis_size(axis))])


def layout(package, rows):
    at = 2 * rows + BITS
    return at + rows * len(package[1])


def pack_body(q, k, v, drop, *refs, peers, per_dev, packages, rows, dim):
    outs = refs[: peers * len(packages)]
    flags, in_sem, flag_sem = refs[peers * len(packages) :]
    me = lax.axis_index("tm")
    zero = jnp.zeros((BITS, dim - drop.shape[3]), BF16)
    plan = [(n, i) for n in range(len(packages)) for i in tuple(range(1, peers)) + (0,)]
    loads = []
    for n, i in plan:
        chunk, asked = packages[n]
        out = outs[n * peers + i]
        parts = [(k, chunk, 0), (v, chunk, rows)]
        parts += [(q, c, (2 + m) * rows + BITS) for m, c in enumerate(asked)]
        for m, (x, c, at) in enumerate(parts):
            where = pl.ds(pl.multiple_of(((me ^ i) * per_dev + c) * dim, dim), dim)
            loads.append(
                pltpu.make_async_copy(x.at[:, where], out.at[pl.ds(at, rows)], in_sem.at[n, i, m])
            )
            loads[-1].start()
    flag_loads = {}
    for n, i in plan:
        head = (me ^ i) * per_dev + packages[n][0]
        flag_loads[n, i] = pltpu.make_async_copy(drop.at[:, head], flags.at[n, i], flag_sem.at[n, i])
        flag_loads[n, i].start()
    for n, i in plan:
        flag_loads[n, i].wait()
        bits = flags[n, i].reshape(BITS, drop.shape[3])
        outs[n * peers + i][2 * rows : 2 * rows + BITS, :] = jnp.concatenate(
            [bits.astype(F32).astype(BF16), zero], axis=1
        )
    for copy in loads:
        copy.wait()


def pack(q, k, v, drop, per_dev, peers, packages):
    rows, width = q.shape
    dim = width // (per_dev * peers)
    sizes = [layout(package, rows) for package in packages for _ in range(peers)]
    flat = pl.pallas_call(
        functools.partial(
            pack_body, peers=peers, per_dev=per_dev, packages=packages, rows=rows, dim=dim
        ),
        in_specs=[HBM] * 4,
        out_specs=[pl.BlockSpec(memory_space=pltpu.VMEM)] * len(sizes),
        scratch_shapes=[
            pltpu.VMEM((len(packages), peers, drop.shape[0]) + drop.shape[2:], drop.dtype),
            pltpu.SemaphoreType.DMA((len(packages), peers, 2 + max(len(p[1]) for p in packages))),
            pltpu.SemaphoreType.DMA((len(packages), peers)),
        ],
        out_shape=[pltpu.VMEM((size, dim), BF16) for size in sizes],
        compiler_params=pltpu.CompilerParams(vmem_limit_bytes=PACK_LIMIT),
        cost_estimate=pl.CostEstimate(
            flops=0, bytes_accessed=4 * sum(sizes) * dim, transcendentals=0
        ),
        name="pack",
    )(q, k, v, drop)
    return [flat[n * peers : (n + 1) * peers] for n in range(len(packages))]


def attend_body(
    lists, column, near, far, *refs, slots, ask_at, rows, tok, samples, factor
):
    asks = refs[:slots]
    outs = refs[slots : 2 * slots]
    keys, vals, q_buf, done, out_sem = refs[2 * slots :]
    dim = near.shape[2]
    half = rows // 2
    span_keys = 2 * rows
    me = lax.axis_index("tm")
    use_near = lists[0, 1] == (lax.axis_index("space") ^ 1)

    for i in range(slots):
        q_buf[me ^ i] = asks[i][ask_at : ask_at + rows, :]

    def part(s, side, at, size):
        slot = me ^ s
        if side == 0:
            return column[slot, at : at + size, :]
        return jnp.where(use_near, near[slot, at : at + size, :], far[slot, at : at + size, :])

    def stage_keys(s):
        for late in range(2):
            for side in range(2):
                at = s * span_keys + (2 * late + side) * half
                keys[at : at + half, :] = part(s, side, late * half, half)

    def stage_values(s):
        for side in range(2):
            turned = part(s, side, 2 * rows, BITS).T
            for f in range(rows // tok):
                value = part(s, side, rows + f * tok, tok)
                late, rest = divmod(f * tok, half)
                at = s * span_keys + (2 * late + side) * half + rest
                for n in range(samples):
                    r = n * (rows // tok) + f
                    keep = jnp.broadcast_to(turned[0:tok, r : r + 1], (tok, dim))
                    vals[at : at + tok, n * dim : (n + 1) * dim] = value * keep

    row_frame = lax.broadcasted_iota(jnp.int32, (rows, rows), 0) // tok
    key_frame = lax.rem(lax.broadcasted_iota(jnp.int32, (rows, rows), 1), half) // tok
    early = key_frame <= row_frame
    late = (key_frame <= row_frame)[:half]
    scale = factor * math.log2(math.e)

    def dot_keys(q, lo, hi):
        return lax.dot_general(
            q, keys[lo:hi, :], (((1,), (1,)), ((), ())), preferred_element_type=F32
        )

    def get_scores(s):
        base = s * span_keys
        q = q_buf[s]
        wide = dot_keys(q, 0, base + rows)
        last = jnp.where(early, wide[:, base:], -1e30)
        wide = jnp.concatenate([wide[:, :base], last], axis=1) if s else last
        tail = jnp.where(late, dot_keys(q[half:], base + rows, base + span_keys), -1e30)
        return wide, tail

    def finish(s, wide, tail):
        base = s * span_keys
        top = jnp.max(wide, axis=1, keepdims=True)
        low_top = jnp.maximum(top[half:], jnp.max(tail, axis=1, keepdims=True))
        top = jnp.concatenate([top[:half], low_top], axis=0)
        w = jnp.exp2((wide - top) * scale)
        w_tail = jnp.exp2((tail - low_top) * scale)
        total = jnp.sum(w, axis=1, keepdims=True)
        low_total = total[half:] + jnp.sum(w_tail, axis=1, keepdims=True)
        acc = jnp.dot(w.astype(BF16), vals[0 : base + rows, :], preferred_element_type=F32)
        more = jnp.dot(
            w_tail.astype(BF16),
            vals[base + rows : base + span_keys, :],
            preferred_element_type=F32,
        )
        for lo, acc_part, sum_part in (
            (0, acc[:half], total[:half]),
            (half, acc[half:] + more, low_total),
        ):
            inv = 1.0 / (keep_rate * sum_part)
            for n in range(samples):
                done[s, n, lo : lo + half, :] = (
                    acc_part[:, n * dim : (n + 1) * dim] * inv
                ).astype(BF16)

    stage_keys(0)
    scores = get_scores(0)
    for s in range(slots):
        if s + 1 < slots:
            stage_keys(s + 1)
            ahead = get_scores(s + 1)
        stage_values(s)
        finish(s, *scores)
        scores = ahead
    sends = [pltpu.make_async_copy(done.at[me ^ i], outs[i], out_sem.at[i]) for i in range(slots)]
    for copy in sends:
        copy.start()
    for copy in sends:
        copy.wait()


def attend(lists, column, near, far, asks, ask_at, rows, tok, samples):
    slots, size, dim = column.shape
    pairs = slots * (slots + 1) // 2
    inside = pl.BlockSpec(memory_space=pltpu.VMEM)
    return pl.pallas_call(
        functools.partial(
            attend_body,
            slots=slots,
            ask_at=ask_at,
            rows=rows,
            tok=tok,
            samples=samples,
            factor=1.0 / math.sqrt(dim),
        ),
        in_specs=[pl.BlockSpec(memory_space=pltpu.SMEM)] + [inside] * (slots + 3),
        out_specs=[ANY] * slots,
        scratch_shapes=[
            pltpu.VMEM((slots * 2 * rows, dim), BF16),
            pltpu.VMEM((slots * 2 * rows, samples * dim), BF16),
            pltpu.VMEM((slots, rows, dim), BF16),
            pltpu.VMEM((slots, samples, rows, dim), BF16),
            pltpu.SemaphoreType.DMA((slots,)),
        ],
        out_shape=[jax.ShapeDtypeStruct((samples, rows, dim), BF16)] * slots,
        compiler_params=pltpu.CompilerParams(vmem_limit_bytes=LIMIT),
        cost_estimate=pl.CostEstimate(
            flops=pairs * rows * 2 * rows * dim * 2 * (1 + samples),
            bytes_accessed=2 * slots * (2 * size + samples * rows) * dim,
            transcendentals=pairs * rows * 2 * rows,
        ),
        name="attend",
    )(lists, column, near, far, *asks)


def put_body(*refs, slots, per_dev, chunk, dim):
    pieces = refs[: len(slots)]
    out, sem = refs[-2:]
    me = lax.axis_index("tm")
    stores = []
    for n, i in enumerate(slots):
        where = pl.ds(pl.multiple_of(((me ^ i) * per_dev + chunk) * dim, dim), dim)
        stores.append(pltpu.make_async_copy(pieces[n], out.at[:, :, where], sem.at[n]))
    for copy in stores:
        copy.start()
    for copy in stores:
        copy.wait()


def put(pieces, slots, prior, shape, per_dev, chunk):
    pieces = [pieces[i] for i in slots]
    peers = len(pieces)
    _, _, dim = pieces[0].shape
    args = pieces if prior is None else pieces + [prior]
    inside = pl.BlockSpec(memory_space=pltpu.VMEM)
    return pl.pallas_call(
        functools.partial(put_body, slots=slots, per_dev=per_dev, chunk=chunk, dim=dim),
        in_specs=[inside] * peers + [ANY] * (len(args) - peers),
        out_specs=ANY,
        scratch_shapes=[pltpu.SemaphoreType.DMA((peers,))],
        out_shape=jax.ShapeDtypeStruct(shape, BF16),
        input_output_aliases={} if prior is None else {peers: 0},
        compiler_params=pltpu.CompilerParams(vmem_limit_bytes=LIMIT),
        cost_estimate=pl.CostEstimate(
            flops=0, bytes_accessed=4 * peers * pieces[0].size, transcendentals=0
        ),
        name="put",
    )(*args)


def per_device(queries, key_rows, value_rows, dropout, tile_lists):
    frame_dev, tok, width = queries.shape
    samples = dropout.shape[0]
    heads = dropout.shape[3]
    rows = frame_dev * tok
    peers = lax.axis_size("tm")
    per_dev = heads // peers
    space = lax.axis_size("space")
    q = queries.reshape(rows, width)
    k = key_rows.reshape(rows, width)
    v = value_rows.reshape(rows, width)
    drop = dropout.transpose(0, 3, 1, 2)
    kept = 2 * rows + BITS

    shape = (samples, rows, width)

    def spread(group):
        moved = [group[0]]
        for i in range(1, peers):
            moved.append(paired(group[i], "tm", lambda n: n ^ i))
        return moved

    def widen(packs):
        column = jnp.stack([x[:kept] for x in packs])
        near = paired(column, "space", lambda n: n ^ 1)
        far = paired(column, "space", lambda n: (((n + 1) ^ 1) - 1) % space)
        return column, near, far

    out = None
    groups = pack(q, k, v, drop, per_dev, peers, PACKAGES[:1])
    groups += pack(q, k, v, drop, per_dev, peers, PACKAGES[1:])
    packs = [spread(groups[n]) for n in range(per_dev)]
    results = []
    for chunk in range(per_dev):
        sides = widen(packs[chunk])
        source = [n for n in range(per_dev) if chunk in PACKAGES[n][1]][0]
        ask_at = kept + rows * PACKAGES[source][1].index(chunk)
        done = attend(tile_lists, *sides, packs[source], ask_at, rows, tok, samples)
        results.append(spread(done))
    for chunk, slots in PUTS:
        out = put(results[chunk], slots, out, shape, per_dev, chunk)
    return out.reshape(samples, frame_dev, tok, width)


PACKAGES = ((0, ()), (1, (0,)), (2, (1, 2)))


PUTS = ((0, (0, 1, 2, 3)), (1, (0, 1, 2, 3)), (2, (0, 1)), (2, (3, 2)))


def solution(mesh):
    placed = (
        P("tm", "space", None),
        P("tm", "space", None),
        P("tm", "space", None),
        P(None, "tm", "space", None),
        P("space", None),
    )
    return jax.shard_map(
        per_device,
        mesh=mesh,
        in_specs=placed,
        out_specs=P(None, "tm", "space", None),
        check_vma=False,
    )
```
